256 devices in a mesh: gx: 32 (over x, z), gy: 8 (over y, core).
Axes of the slice: x: 4, y: 4, z: 8, core: 2. Of those that a mesh axis runs over, the one named last changes fastest.
Arguments:
- features: bfloat16 [2097152, 64], P(('gx', 'gy')), may hold values from -6 to 6
- conv_weight: bfloat16 [27, 64, 64], replicated, may hold values from -0.15625 to 0.15625
- down_weight: bfloat16 [8, 64, 128], replicated, may hold values from -0.375 to 0.375
- kernel_map: int32 [27, 16384], P(None, ('gx', 'gy')), may hold values from 0 to 128, as said below
- halo_rows: int32 [8, 2048], P(None, ('gx', 'gy')), may hold values from 0 to 63
- send_rows: int32 [32, 131072], P(None, ('gx', 'gy')), may hold values from 0 to 8192, as said below
- send_sub: int32 [32, 131072], P(None, ('gx', 'gy')), may hold values from 0 to 7
- recv_coarse: int32 [32, 131072], P(None, ('gx', 'gy')), may hold values from 0 to 2047
Outputs:
- refined: bfloat16 [2097152, 64], P(('gx', 'gy'))
- coarse: bfloat16 [524288, 128], P(('gx', 'gy'))
The draws below stay inside these ranges and needn't reach their ends.
Inputs may be any that keep to these rules, and one draw needn't show every extreme that they name: `kernel_map`: entries below 64 name local blocks, the next 64 name the received blocks of directions 0 to 7 in order, 128 means no neighbour; offset 13 maps every block to itself. `send_rows`: each local row below 8192 stands in exactly one slot of its slab; 8192 marks an empty slot; one hash owner of each slab gets all 512 of its slots filled.
All inputs are finite; a program needn't handle non-finite values.
Results may differ from the reference program's by a relative error of at most 0.0047.
Values may be sent and summed in bfloat16 or wider, within the bound.
A program may use at most 128 MiB of HBM per device.

```python
import jax
import jax.numpy as jnp
from jax import lax

CH = 64
COUT = 128
KOFF = 27
BLOCK = 128
V_DEV = 8192
HALO = 1024
CAP = 512
CDEV = 2048
ROWS = 2097152
N_GX = 32
N_GY = 8


def draw_kernel_map(key, part):
    processor_list = N_GX * N_GY
    block_total = V_DEV // BLOCK
    extent = (V_DEV + 8 * HALO) // BLOCK
    first_key, second_key = jax.random.split(key)
    pointer = jax.random.randint(first_key, (KOFF, processor_list * block_total), 0, extent)
    absent = jax.random.randint(second_key, (KOFF, processor_list * block_total), 0, 2)
    kernel_table = jnp.where(absent == 1, extent, pointer).astype(jnp.int32)
    centre = jnp.tile(jnp.arange(block_total, dtype=jnp.int32), processor_list)
    return kernel_table.at[13].set(centre)


def slab_slots(key):
    capacity = 2 * V_DEV // N_GX
    first_key, second_key, third_key = jax.random.split(key, 3)
    sorted_sequence = jax.random.permutation(first_key, V_DEV).astype(jnp.int32)
    busiest = jax.random.randint(second_key, (), 0, N_GX)
    slots_table = jnp.full((N_GX, capacity), V_DEV, jnp.int32)
    slots_table = slots_table.at[busiest].set(sorted_sequence[:capacity])
    remaining = V_DEV - capacity
    other_grid = (N_GX - 1) * capacity
    chosen_slots = jax.random.permutation(third_key, other_grid)[:remaining].astype(jnp.int32)
    others = chosen_slots // capacity
    peer_index = others + (others >= busiest).astype(jnp.int32)
    slot_index = chosen_slots % capacity
    return slots_table.at[peer_index, slot_index].set(sorted_sequence[capacity:])


def draw_send_rows(key, part):
    processor_list = N_GX * N_GY
    capacity = 2 * V_DEV // N_GX
    stacked = jax.vmap(slab_slots)(jax.random.split(key, processor_list))
    return stacked.transpose(1, 0, 2).reshape(N_GX, processor_list * capacity).astype(jnp.int32)


def set_ends(result, stream_key, least, high):
    shape = result.shape
    index_at = [jax.random.randint(jax.random.fold_in(stream_key, axis), (), 0, shape[axis]) for axis in range(len(shape))]
    result = result.at[tuple(index_at)].set(least)
    longest = shape.index(max(shape))
    index_at[longest] = (index_at[longest] + 1) % shape[longest]
    return result.at[tuple(index_at)].set(high)


def level_of(stream_key, dims, shards, least, top_value):
    gain = 1.0
    for dim, parts in shards:
        steps = jax.random.uniform(jax.random.fold_in(jax.random.fold_in(stream_key, 6), dim), (parts,), jnp.float32, least / len(shards), top_value / len(shards))
        gain = gain * jnp.repeat(jnp.exp(steps), dims[dim] // parts).reshape((-1,) + (1,) * (len(dims) - 1 - dim))
    return gain


def centred(key, dims, scale, reach, shards=(), kind=jnp.bfloat16):
    array = jax.random.normal(key, dims, jnp.float32) * scale
    if len(shards) > 0:
        array = level_of(key, dims, shards, -0.22, 0.18) * array
    return jnp.clip(array, min=-reach, max=reach).astype(kind)


def setup_inputs(seed: int = 0) -> dict:
    key_list = jax.random.split(jax.random.key(seed), 9)
    return {
        "features": centred(key_list[0], (ROWS, CH), 1.0, 6.0, ((0, 256),)),
        "conv_weight": centred(key_list[1], (KOFF, CH, CH), (KOFF * CH) ** -0.5, 0.15625),
        "down_weight": centred(key_list[2], (8, CH, COUT), (4 * CH) ** -0.5, 0.375),
        "kernel_map": draw_kernel_map(jax.random.fold_in(key_list[8], 71), 0),
        "halo_rows": set_ends(jax.random.randint(key_list[4], (8, HALO // BLOCK * N_GX * N_GY), 0, V_DEV // BLOCK), jax.random.fold_in(key_list[4], 1), 0, (V_DEV // BLOCK) - 1).astype(jnp.int32),
        "send_rows": draw_send_rows(jax.random.fold_in(key_list[8], 71), 0),
        "send_sub": set_ends(jax.random.randint(key_list[6], (N_GX, CAP * N_GX * N_GY), 0, 8), jax.random.fold_in(key_list[6], 1), 0, 7).astype(jnp.int32),
        "recv_coarse": set_ends(jax.random.randint(key_list[7], (N_GX, CAP * N_GX * N_GY), 0, CDEV), jax.random.fold_in(key_list[7], 1), 0, CDEV - 1).astype(jnp.int32),
    }


DIRECTIONS = ((-1, -1), (-1, 0), (-1, 1), (0, -1), (0, 1), (1, -1), (1, 0), (1, 1))


def reference(features, conv_weight, down_weight, kernel_map, halo_rows, send_rows, send_sub, recv_coarse):
    processor_list = N_GX * N_GY
    block_total = V_DEV // BLOCK
    halo_blocks = HALO // BLOCK
    slabs = features.reshape(N_GX, N_GY, V_DEV, CH)
    slab_blocks = features.reshape(N_GX, N_GY, block_total, BLOCK, CH)
    halo_lists = halo_rows.reshape(8, N_GX, N_GY, halo_blocks).transpose(1, 2, 0, 3)
    outgoing = jax.vmap(jax.vmap(lambda source_slab, chosen: source_slab[chosen]))(slab_blocks, halo_lists)
    outgoing = outgoing.reshape(N_GX, N_GY, 8, HALO, CH)
    padded = jnp.pad(outgoing, ((1, 1), (1, 1), (0, 0), (0, 0), (0, 0)))
    received = jnp.stack([padded[1 - shift_x:1 - shift_x + N_GX, 1 - shift_y:1 - shift_y + N_GY, number] for number, (shift_x, shift_y) in enumerate(DIRECTIONS)], axis=2)
    tables = jnp.concatenate([slabs, received.reshape(N_GX, N_GY, 8 * HALO, CH), jnp.zeros((N_GX, N_GY, BLOCK, CH), features.dtype)], axis=2)
    tables = tables.reshape(processor_list, (V_DEV + 8 * HALO) // BLOCK + 1, BLOCK, CH)
    offsets = kernel_map.reshape(KOFF, processor_list, block_total).transpose(1, 0, 2)
    weights = conv_weight.astype(jnp.float32)

    def convolve(operands):
        lookup_table, displaced_blocks = operands
        picked = lookup_table[displaced_blocks].astype(jnp.float32)
        summed_conv = jnp.einsum("knbc,kcd->nbd", picked, weights, precision=lax.Precision.HIGHEST)
        return jax.nn.relu(summed_conv.reshape(V_DEV, CH)).astype(jnp.bfloat16)

    refined = lax.map(convolve, (tables, offsets))
    padded_fine = jnp.concatenate([refined, jnp.zeros((processor_list, 1, CH), jnp.bfloat16)], axis=1).reshape(N_GX, N_GY, V_DEV + 1, CH)
    sender_rows = send_rows.reshape(N_GX, N_GX, N_GY, CAP).transpose(1, 2, 0, 3)
    sender_sub = send_sub.reshape(N_GX, N_GX, N_GY, CAP).transpose(1, 2, 0, 3)
    receiver_coarse = recv_coarse.reshape(N_GX, N_GX, N_GY, CAP).transpose(1, 2, 0, 3)
    down_flat = down_weight.reshape(8 * CH, COUT).astype(jnp.float32)

    def stride_reduce(processor_index):
        destination_x = processor_index // N_GY
        target_y = processor_index % N_GY
        sources = padded_fine[:, target_y]
        chosen_rows = sender_rows[:, target_y, destination_x]
        sub_codes = sender_sub[:, target_y, destination_x]
        picked = jax.vmap(lambda source_slab, chosen: source_slab[chosen])(sources, chosen_rows)
        segment = receiver_coarse[destination_x, target_y] * 8 + sub_codes
        summed = jax.ops.segment_sum(picked.reshape(-1, CH).astype(jnp.float32), segment.reshape(-1), num_segments=CDEV * 8)
        product = jnp.dot(summed.reshape(CDEV, 8 * CH), down_flat, precision=lax.Precision.HIGHEST)
        return product.astype(jnp.bfloat16)

    coarse = lax.map(stride_reduce, jnp.arange(processor_list, dtype=jnp.int32))
    return refined.reshape(processor_list * V_DEV, CH), coarse.reshape(processor_list * CDEV, COUT)
```

```python
import functools

import jax
import jax.numpy as jnp
from jax import lax
from jax.experimental import pallas as pl
from jax.experimental.pallas import tpu as pltpu
from jax.sharding import PartitionSpec as P

MESH = pl.DeviceIdType.MESH
BLOCK = 128
DIRECTIONS = ((-1, -1), (-1, 0), (-1, 1), (0, -1), (0, 1), (1, -1), (1, 0), (1, 1))
VMEM_LIMIT = 60 * 1024 * 1024


def pack_kernel(halo_ref, feat_ref, out_ref):
    channels = feat_ref.shape[0]
    directions, per_direction = halo_ref.shape

    @pl.loop(0, directions)
    def _(j):
        for m in range(per_direction):
            column = pl.multiple_of(halo_ref[j, m] * BLOCK, BLOCK)
            out_ref[j, m * channels : (m + 1) * channels, :] = feat_ref[:, pl.ds(column, BLOCK)]


def halo_kernel(n_gx, n_gy, sent, out_ref, send_sem, recv_sem):
    gx, gy = lax.axis_index("gx"), lax.axis_index("gy")
    barrier = pltpu.get_barrier_semaphore()
    for dx, dy in DIRECTIONS:
        peer = (lax.rem(gx + dx + n_gx, n_gx), lax.rem(gy + dy + n_gy, n_gy))
        pl.semaphore_signal(barrier, inc=1, device_id=peer, device_id_type=MESH)
    pl.semaphore_wait(barrier, len(DIRECTIONS))

    def inside(x, y):
        return (x >= 0) & (x < n_gx) & (y >= 0) & (y < n_gy)

    def copy(j, peer):
        return pltpu.make_async_remote_copy(
            src_ref=sent.at[j],
            dst_ref=out_ref.at[j],
            send_sem=send_sem.at[j],
            recv_sem=recv_sem.at[j],
            device_id=peer,
            device_id_type=MESH,
        )

    for j, (dx, dy) in enumerate(DIRECTIONS):
        @pl.when(inside(gx + dx, gy + dy))
        def _():
            copy(j, (gx + dx, gy + dy)).start()

    for j, (dx, dy) in enumerate(DIRECTIONS):
        @pl.when(jnp.logical_not(inside(gx - dx, gy - dy)))
        def _():
            out_ref[j] = jnp.zeros(out_ref.shape[1:], out_ref.dtype)

    for j, (dx, dy) in enumerate(DIRECTIONS):
        @pl.when(inside(gx - dx, gy - dy))
        def _():
            copy(j, (gx, gy)).wait_recv()

        @pl.when(inside(gx + dx, gy + dy))
        def _():
            copy(j, (gx, gy)).wait_send()


def exchange_halo(feat_t, halo_rows, n_gx, n_gy):
    channels = feat_t.shape[0]
    directions, per_direction = halo_rows.shape
    page = (directions, per_direction * channels, BLOCK)
    vmem = pl.BlockSpec(memory_space=pltpu.VMEM)
    sent = pl.pallas_call(
        pack_kernel,
        out_shape=jax.ShapeDtypeStruct(page, feat_t.dtype),
        in_specs=[pl.BlockSpec(memory_space=pltpu.SMEM), vmem],
        out_specs=vmem,
        name="pack",
    )(halo_rows, feat_t)
    return pl.pallas_call(
        functools.partial(halo_kernel, n_gx, n_gy),
        out_shape=jax.ShapeDtypeStruct(page, feat_t.dtype),
        in_specs=[vmem],
        out_specs=vmem,
        scratch_shapes=[
            pltpu.SemaphoreType.DMA((directions,)),
            pltpu.SemaphoreType.DMA((directions,)),
        ],
        compiler_params=pltpu.CompilerParams(collective_id=0, has_side_effects=True),
        name="halo",
    )(sent)


def doubled_rows(block):
    wide = jnp.concatenate([block, block], axis=0)
    return jnp.transpose(wide)


def conv_kernel(
    group, map_ref, rows_ref, feat_ref, halo_ref, w_ref, out_ref, slot_ref,
    table, weights, lhs, fine, stage,
):
    offsets, blocks = map_ref.shape
    channels, voxels = feat_ref.shape
    halo_blocks = halo_ref.shape[0] // channels
    peers, half, lanes = slot_ref.shape
    pairs = (offsets + 1) // 2
    low = lax.broadcasted_iota(jnp.int32, (BLOCK, lanes), 1) < channels

    weights[...] = jnp.zeros(weights.shape, weights.dtype)
    weights[: offsets * channels, :] = jnp.concatenate([w_ref[...], w_ref[...]], axis=1)

    @pl.loop(0, blocks)
    def _(i):
        column = pl.multiple_of(i * BLOCK, BLOCK)
        table[pl.ds(column, BLOCK), :] = doubled_rows(feat_ref[:, pl.ds(column, BLOCK)])

    @pl.loop(0, halo_blocks)
    def _(i):
        row = pl.multiple_of((blocks + i) * BLOCK, BLOCK)
        source = pl.multiple_of(i * channels, channels)
        table[pl.ds(row, BLOCK), :] = doubled_rows(halo_ref[pl.ds(source, channels), :])

    empty = (blocks + halo_blocks) * BLOCK
    table[empty : empty + BLOCK, :] = jnp.zeros((BLOCK, lanes), table.dtype)
    fine[voxels : voxels + 8, :] = jnp.zeros((8, lanes), fine.dtype)

    def pick(k, i):
        return table[pl.ds(pl.multiple_of(map_ref[k, i] * BLOCK, BLOCK), BLOCK), :]

    @pl.loop(0, blocks // group)
    def _(g):
        for b in range(group):
            i = g * group + b
            for pair in range(pairs):
                first = pick(2 * pair, i)
                if 2 * pair + 1 < offsets:
                    both = jnp.where(low, first, pick(2 * pair + 1, i))
                else:
                    both = jnp.where(low, first, jnp.zeros_like(first))
                lhs[b * BLOCK : (b + 1) * BLOCK, pair * lanes : (pair + 1) * lanes] = both
        total = jnp.dot(lhs[...], weights[...], preferred_element_type=jnp.float32)
        refined = jnp.maximum(total, 0.0).astype(jnp.bfloat16).astype(jnp.float32)
        start = pl.multiple_of(g * group * BLOCK, group * BLOCK)
        fine[pl.ds(start, group * BLOCK), :] = refined
        for b in range(group):
            block = refined[b * BLOCK : (b + 1) * BLOCK, :]
            column = pl.multiple_of(start + b * BLOCK, BLOCK)
            out_ref[:, pl.ds(column, BLOCK)] = jnp.transpose(block)[:channels, :].astype(
                out_ref.dtype
            )

    low_row = lax.broadcasted_iota(jnp.int32, (1, lanes), 1) < channels

    @pl.loop(0, peers)
    def _(p):
        for c in range(half):
            first = fine[pl.ds(rows_ref[p, c], 1), :]
            second = fine[pl.ds(rows_ref[p, half + c], 1), :]
            stage[c : c + 1, :] = jnp.where(low_row, first, second)
        slot_ref[p] = stage[...].astype(slot_ref.dtype)


def convolve(feat_t, halo, conv_weight, kernel_map, send_rows):
    channels, voxels = feat_t.shape
    offsets, blocks = kernel_map.shape
    peers, capacity = send_rows.shape
    group = 8
    pairs = (offsets + 1) // 2
    lanes = 2 * channels
    halo_blocks = halo.shape[0] // channels
    vmem = pl.BlockSpec(memory_space=pltpu.VMEM)
    smem = pl.BlockSpec(memory_space=pltpu.SMEM)
    return pl.pallas_call(
        functools.partial(conv_kernel, group),
        out_shape=(
            jax.ShapeDtypeStruct((channels, voxels), jnp.bfloat16),
            jax.ShapeDtypeStruct((peers, capacity // 2, lanes), jnp.bfloat16),
        ),
        in_specs=[smem, smem, vmem, vmem, vmem],
        out_specs=(vmem, vmem),
        scratch_shapes=[
            pltpu.VMEM(((blocks + halo_blocks + 1) * BLOCK, lanes), jnp.bfloat16),
            pltpu.VMEM((pairs * lanes, lanes), jnp.bfloat16),
            pltpu.VMEM((group * BLOCK, pairs * lanes), jnp.bfloat16),
            pltpu.VMEM((voxels + 8, lanes), jnp.float32),
            pltpu.VMEM((capacity // 2, lanes), jnp.float32),
        ],
        compiler_params=pltpu.CompilerParams(vmem_limit_bytes=VMEM_LIMIT),
        name="convolve",
    )(kernel_map, send_rows, feat_t, halo, conv_weight.reshape(offsets * channels, channels))


def reduce_kernel(slot_ref, sub_ref, coarse_ref, w_ref, out_ref, wide, placed, terms, hot, total):
    peers, half, lanes = slot_ref.shape
    subs, channels, width = w_ref.shape
    coarse_count = out_ref.shape[0]
    wide[...] = jnp.zeros(wide.shape, wide.dtype)
    for s in range(subs):
        wide[s * lanes : s * lanes + channels, :width] = w_ref[s]
        wide[s * lanes + channels : (s + 1) * lanes, width:] = w_ref[s]
    total[...] = jnp.zeros(total.shape, total.dtype)
    ids = lax.broadcasted_iota(jnp.int32, (BLOCK, 2 * half), 0).astype(jnp.bfloat16)

    @pl.loop(0, peers)
    def _(a):
        code = sub_ref[pl.ds(a, 1), :].astype(jnp.float32)
        spread = jnp.concatenate(
            [
                jnp.broadcast_to(code[:, :half], (channels, half)),
                jnp.broadcast_to(code[:, half:], (channels, half)),
            ],
            axis=0,
        )
        column = jnp.transpose(spread).astype(jnp.bfloat16)
        rows = slot_ref[a]
        for s in range(subs):
            placed[:, s * lanes : (s + 1) * lanes] = jnp.where(
                column == jnp.bfloat16(s), rows, jnp.zeros_like(rows)
            )
        product = jnp.dot(placed[...], wide[...], preferred_element_type=jnp.float32)
        high = product.astype(jnp.bfloat16)
        rest = (product - high.astype(jnp.float32)).astype(jnp.bfloat16)
        terms[:half, :width] = high[:, :width]
        terms[:half, width:] = rest[:, :width]
        terms[half:, :width] = high[:, width:]
        terms[half:, width:] = rest[:, width:]
        target = coarse_ref[pl.ds(a, 1), :]
        upper = target // BLOCK
        lower = target - upper * BLOCK
        for h in range(coarse_count // BLOCK):
            wanted = jnp.where(upper == h, lower, -1).astype(jnp.float32).astype(jnp.bfloat16)
            hot[h * BLOCK : (h + 1) * BLOCK, :] = jnp.where(
                ids == wanted, jnp.bfloat16(1), jnp.bfloat16(0)
            )
        total[...] += jnp.dot(hot[...], terms[...], preferred_element_type=jnp.float32)

    out_ref[...] = (total[:, :width] + total[:, width:]).astype(out_ref.dtype)


def reduce_coarse(slots, subs, recv_coarse, down_weight, coarse_count):
    peers, half, lanes = slots.shape
    width = down_weight.shape[2]
    vmem = pl.BlockSpec(memory_space=pltpu.VMEM)
    return pl.pallas_call(
        reduce_kernel,
        out_shape=jax.ShapeDtypeStruct((coarse_count, width), jnp.bfloat16),
        in_specs=[vmem] * 4,
        out_specs=vmem,
        scratch_shapes=[
            pltpu.VMEM((down_weight.shape[0] * lanes, 2 * width), jnp.bfloat16),
            pltpu.VMEM((half, down_weight.shape[0] * lanes), jnp.bfloat16),
            pltpu.VMEM((2 * half, 2 * width), jnp.bfloat16),
            pltpu.VMEM((coarse_count, 2 * half), jnp.bfloat16),
            pltpu.VMEM((coarse_count, 2 * width), jnp.float32),
        ],
        compiler_params=pltpu.CompilerParams(vmem_limit_bytes=VMEM_LIMIT),
        name="reduce",
    )(slots, subs, recv_coarse, down_weight)


def on_device(
    n_gx, n_gy,
    features, conv_weight, down_weight, kernel_map, halo_rows, send_rows, send_sub, recv_coarse,
):
    voxels, channels = features.shape
    subs = lax.all_to_all(send_sub, "gx", split_axis=0, concat_axis=0, tiled=True)
    feat_t = features.T
    halo = exchange_halo(feat_t, halo_rows, n_gx, n_gy).reshape(-1, BLOCK)
    refined_t, slots = convolve(feat_t, halo, conv_weight, kernel_map, send_rows)
    landed = lax.all_to_all(slots, "gx", split_axis=0, concat_axis=0, tiled=True)
    coarse = reduce_coarse(landed, subs, recv_coarse, down_weight, voxels // 4)
    return refined_t.T, coarse


def solution(mesh):
    split = P(None, ("gx", "gy"))
    return jax.shard_map(
        functools.partial(on_device, mesh.shape["gx"], mesh.shape["gy"]),
        mesh=mesh,
        in_specs=(P(("gx", "gy"), None), P(), P(), split, split, split, split, split),
        out_specs=(P(("gx", "gy"), None), P(("gx", "gy"), None)),
        check_vma=False,
    )
```

```python
import functools

import jax
import jax.numpy as jnp
from jax import lax
from jax.experimental import pallas as pl
from jax.experimental.pallas import tpu as pltpu
from jax.sharding import PartitionSpec as P

MESH = pl.DeviceIdType.MESH
BLOCK = 128
DIRECTIONS = ((-1, -1), (-1, 0), (-1, 1), (0, -1), (0, 1), (1, -1), (1, 0), (1, 1))
VMEM_LIMIT = 60 * 1024 * 1024


def pack_kernel(halo_ref, feat_ref, out_ref):
    channels = feat_ref.shape[0]
    directions, per_direction = halo_ref.shape

    @pl.loop(0, directions)
    def _(j):
        for m in range(per_direction):
            column = pl.multiple_of(halo_ref[j, m] * BLOCK, BLOCK)
            out_ref[j, m * channels : (m + 1) * channels, :] = feat_ref[:, pl.ds(column, BLOCK)]


def halo_kernel(n_gx, n_gy, sent, out_ref, send_sem, recv_sem):
    gx, gy = lax.axis_index("gx"), lax.axis_index("gy")
    barrier = pltpu.get_barrier_semaphore()
    for dx, dy in DIRECTIONS:
        peer = (lax.rem(gx + dx + n_gx, n_gx), lax.rem(gy + dy + n_gy, n_gy))
        pl.semaphore_signal(barrier, inc=1, device_id=peer, device_id_type=MESH)
    pl.semaphore_wait(barrier, len(DIRECTIONS))

    def inside(x, y):
        return (x >= 0) & (x < n_gx) & (y >= 0) & (y < n_gy)

    def copy(j, peer):
        return pltpu.make_async_remote_copy(
            src_ref=sent.at[j],
            dst_ref=out_ref.at[j],
            send_sem=send_sem.at[j],
            recv_sem=recv_sem.at[j],
            device_id=peer,
            device_id_type=MESH,
        )

    for j, (dx, dy) in enumerate(DIRECTIONS):
        @pl.when(inside(gx + dx, gy + dy))
        def _():
            copy(j, (gx + dx, gy + dy)).start()

    for j, (dx, dy) in enumerate(DIRECTIONS):
        @pl.when(jnp.logical_not(inside(gx - dx, gy - dy)))
        def _():
            out_ref[j] = jnp.zeros(out_ref.shape[1:], out_ref.dtype)

    for j, (dx, dy) in enumerate(DIRECTIONS):
        @pl.when(inside(gx - dx, gy - dy))
        def _():
            copy(j, (gx, gy)).wait_recv()

        @pl.when(inside(gx + dx, gy + dy))
        def _():
            copy(j, (gx, gy)).wait_send()


def exchange_halo(feat_t, halo_rows, n_gx, n_gy):
    channels = feat_t.shape[0]
    directions, per_direction = halo_rows.shape
    page = (directions, per_direction * channels, BLOCK)
    vmem = pl.BlockSpec(memory_space=pltpu.VMEM)
    sent = pl.pallas_call(
        pack_kernel,
        out_shape=jax.ShapeDtypeStruct(page, feat_t.dtype),
        in_specs=[pl.BlockSpec(memory_space=pltpu.SMEM), vmem],
        out_specs=vmem,
        name="pack",
    )(halo_rows, feat_t)
    return pl.pallas_call(
        functools.partial(halo_kernel, n_gx, n_gy),
        out_shape=jax.ShapeDtypeStruct(page, feat_t.dtype),
        in_specs=[vmem],
        out_specs=vmem,
        scratch_shapes=[
            pltpu.SemaphoreType.DMA((directions,)),
            pltpu.SemaphoreType.DMA((directions,)),
        ],
        compiler_params=pltpu.CompilerParams(collective_id=0, has_side_effects=True),
        name="halo",
    )(sent)


def doubled_rows(block):
    wide = jnp.concatenate([block, block], axis=0)
    return jnp.transpose(wide)


def conv_kernel(
    group, map_ref, rows_ref, feat_ref, halo_ref, w_ref, out_ref, slot_ref,
    table, weights, lhs, fine, stage,
):
    offsets, blocks = map_ref.shape
    channels, voxels = feat_ref.shape
    halo_blocks = halo_ref.shape[0] // channels
    peers, half, lanes = slot_ref.shape
    pairs = (offsets + 1) // 2
    low = lax.broadcasted_iota(jnp.int32, (BLOCK, lanes), 1) < channels

    weights[...] = jnp.zeros(weights.shape, weights.dtype)
    weights[: offsets * channels, :] = jnp.concatenate([w_ref[...], w_ref[...]], axis=1)

    @pl.loop(0, blocks)
    def _(i):
        column = pl.multiple_of(i * BLOCK, BLOCK)
        table[pl.ds(column, BLOCK), :] = doubled_rows(feat_ref[:, pl.ds(column, BLOCK)])

    @pl.loop(0, halo_blocks)
    def _(i):
        row = pl.multiple_of((blocks + i) * BLOCK, BLOCK)
        source = pl.multiple_of(i * channels, channels)
        table[pl.ds(row, BLOCK), :] = doubled_rows(halo_ref[pl.ds(source, channels), :])

    empty = (blocks + halo_blocks) * BLOCK
    table[empty : empty + BLOCK, :] = jnp.zeros((BLOCK, lanes), table.dtype)
    fine[voxels : voxels + 8, :] = jnp.zeros((8, lanes), fine.dtype)

    def pick(k, i):
        return table[pl.ds(pl.multiple_of(map_ref[k, i] * BLOCK, BLOCK), BLOCK), :]

    @pl.loop(0, blocks // group)
    def _(g):
        for b in range(group):
            i = g * group + b
            for pair in range(pairs):
                first = pick(2 * pair, i)
                if 2 * pair + 1 < offsets:
                    both = jnp.where(low, first, pick(2 * pair + 1, i))
                else:
                    both = jnp.where(low, first, jnp.zeros_like(first))
                lhs[b * BLOCK : (b + 1) * BLOCK, pair * lanes : (pair + 1) * lanes] = both
        total = jnp.dot(lhs[...], weights[...], preferred_element_type=jnp.float32)
        refined = jnp.maximum(total, 0.0).astype(jnp.bfloat16).astype(jnp.float32)
        start = pl.multiple_of(g * group * BLOCK, group * BLOCK)
        fine[pl.ds(start, group * BLOCK), :] = refined
        for b in range(group):
            block = refined[b * BLOCK : (b + 1) * BLOCK, :]
            column = pl.multiple_of(start + b * BLOCK, BLOCK)
            out_ref[:, pl.ds(column, BLOCK)] = jnp.transpose(block)[:channels, :].astype(
                out_ref.dtype
            )

    low_row = lax.broadcasted_iota(jnp.int32, (1, lanes), 1) < channels

    @pl.loop(0, peers)
    def _(p):
        for c in range(half):
            first = fine[pl.ds(rows_ref[p, c], 1), :]
            second = fine[pl.ds(rows_ref[p, half + c], 1), :]
            stage[c : c + 1, :] = jnp.where(low_row, first, second)
        slot_ref[p] = stage[...].astype(slot_ref.dtype)


def convolve(feat_t, halo, conv_weight, kernel_map, send_rows):
    channels, voxels = feat_t.shape
    offsets, blocks = kernel_map.shape
    peers, capacity = send_rows.shape
    group = 8
    pairs = (offsets + 1) // 2
    lanes = 2 * channels
    halo_blocks = halo.shape[0] // channels
    vmem = pl.BlockSpec(memory_space=pltpu.VMEM)
    smem = pl.BlockSpec(memory_space=pltpu.SMEM)
    return pl.pallas_call(
        functools.partial(conv_kernel, group),
        out_shape=(
            jax.ShapeDtypeStruct((channels, voxels), jnp.bfloat16),
            jax.ShapeDtypeStruct((peers, capacity // 2, lanes), jnp.bfloat16),
        ),
        in_specs=[smem, smem, vmem, vmem, vmem],
        out_specs=(vmem, vmem),
        scratch_shapes=[
            pltpu.VMEM(((blocks + halo_blocks + 1) * BLOCK, lanes), jnp.bfloat16),
            pltpu.VMEM((pairs * lanes, lanes), jnp.bfloat16),
            pltpu.VMEM((group * BLOCK, pairs * lanes), jnp.bfloat16),
            pltpu.VMEM((voxels + 8, lanes), jnp.float32),
            pltpu.VMEM((capacity // 2, lanes), jnp.float32),
        ],
        compiler_params=pltpu.CompilerParams(vmem_limit_bytes=VMEM_LIMIT),
        name="convolve",
    )(kernel_map, send_rows, feat_t, halo, conv_weight.reshape(offsets * channels, channels))


def torus_peer(me, depth, n_gx, step):
    spread = lax.rem(step, depth)
    odd = lax.rem(spread, 2)
    ahead = odd * ((spread + 1) // 2) + (1 - odd) * (depth - spread // 2)
    across, along = me // depth, lax.rem(me, depth)
    wide = n_gx // depth
    there = lax.rem(across + step // depth, wide)
    back = lax.rem(across - step // depth + wide, wide)
    to = there * depth + lax.rem(along + ahead, depth)
    source = back * depth + lax.rem(along - ahead + depth, depth)
    return to, source


def exchange_kernel(
    n_gx, depth, window,
    slot_ref, sub_ref, coarse_ref, w_ref, out_ref,
    landed, codes, wide, placed, terms, hot, total,
    row_send, row_recv, code_send, code_recv, own_sem,
):
    me, gy = lax.axis_index("gx"), lax.axis_index("gy")
    peers, half, lanes = slot_ref.shape
    subs, channels, width = w_ref.shape
    coarse_count = out_ref.shape[0]

    barrier = pltpu.get_barrier_semaphore()

    @pl.loop(1, n_gx)
    def _(step):
        to, source = torus_peer(me, depth, n_gx, step)
        pl.semaphore_signal(barrier, inc=1, device_id=(to, gy), device_id_type=MESH)

    own_rows = pltpu.make_async_copy(slot_ref.at[me], landed.at[0], own_sem.at[0])
    own_codes = pltpu.make_async_copy(sub_ref.at[me], codes.at[0], own_sem.at[1])
    own_rows.start()
    own_codes.start()

    wide[...] = jnp.zeros(wide.shape, wide.dtype)
    for s in range(subs):
        wide[s * lanes : s * lanes + channels, :width] = w_ref[s]
        wide[s * lanes + channels : (s + 1) * lanes, width:] = w_ref[s]
    total[...] = jnp.zeros(total.shape, total.dtype)
    ids = lax.broadcasted_iota(jnp.int32, (BLOCK, 2 * half), 0).astype(jnp.bfloat16)
    pl.semaphore_wait(barrier, n_gx - 1)

    def rows_copy(step, to):
        return pltpu.make_async_remote_copy(
            src_ref=slot_ref.at[to],
            dst_ref=landed.at[step],
            send_sem=row_send.at[step],
            recv_sem=row_recv.at[step],
            device_id=(to, gy),
            device_id_type=MESH,
        )

    def codes_copy(step, to):
        return pltpu.make_async_remote_copy(
            src_ref=sub_ref.at[to],
            dst_ref=codes.at[step],
            send_sem=code_send.at[step],
            recv_sem=code_recv.at[step],
            device_id=(to, gy),
            device_id_type=MESH,
        )

    def send(step):
        to, source = torus_peer(me, depth, n_gx, step)
        codes_copy(step, to).start()
        rows_copy(step, to).start()

    def reduce(step):
        to, source = torus_peer(me, depth, n_gx, step)
        code = codes[step].astype(jnp.float32)
        spread = jnp.concatenate(
            [
                jnp.broadcast_to(code[:, :half], (channels, half)),
                jnp.broadcast_to(code[:, half:], (channels, half)),
            ],
            axis=0,
        )
        column = jnp.transpose(spread).astype(jnp.bfloat16)
        rows = landed[step]
        for s in range(subs):
            placed[:, s * lanes : (s + 1) * lanes] = jnp.where(
                column == jnp.bfloat16(s), rows, jnp.zeros_like(rows)
            )
        product = jnp.dot(placed[...], wide[...], preferred_element_type=jnp.float32)
        high = product.astype(jnp.bfloat16)
        rest = (product - high.astype(jnp.float32)).astype(jnp.bfloat16)
        terms[:half, :width] = high[:, :width]
        terms[:half, width:] = rest[:, :width]
        terms[half:, :width] = high[:, width:]
        terms[half:, width:] = rest[:, width:]
        target = coarse_ref[pl.ds(source, 1), :]
        upper = target // BLOCK
        lower = target - upper * BLOCK
        for h in range(coarse_count // BLOCK):
            wanted = jnp.where(upper == h, lower, -1).astype(jnp.float32).astype(jnp.bfloat16)
            hot[h * BLOCK : (h + 1) * BLOCK, :] = jnp.where(
                ids == wanted, jnp.bfloat16(1), jnp.bfloat16(0)
            )
        total[...] += jnp.dot(hot[...], terms[...], preferred_element_type=jnp.float32)

    @pl.loop(1, window)
    def _(step):
        send(step)

    own_rows.wait()
    own_codes.wait()

    @pl.loop(0, n_gx)
    def _(step):
        @pl.when(step + window < n_gx)
        def _():
            send(step + window)

        @pl.when(step > 0)
        def _():
            codes_copy(step, me).wait_recv()
            rows_copy(step, me).wait_recv()

        reduce(step)

    @pl.loop(1, n_gx)
    def _(step):
        codes_copy(step, me).wait_send()
        rows_copy(step, me).wait_send()

    out_ref[...] = (total[:, :width] + total[:, width:]).astype(out_ref.dtype)


def exchange_and_reduce(slots, send_sub, recv_coarse, down_weight, coarse_count, n_gx):
    peers, half, lanes = slots.shape
    width = down_weight.shape[2]
    depth = 8
    window = 13
    vmem = pl.BlockSpec(memory_space=pltpu.VMEM)
    return pl.pallas_call(
        functools.partial(exchange_kernel, n_gx, depth, window),
        out_shape=jax.ShapeDtypeStruct((coarse_count, width), jnp.bfloat16),
        in_specs=[pl.BlockSpec(memory_space=pl.ANY), vmem, vmem, vmem],
        out_specs=vmem,
        scratch_shapes=[
            pltpu.VMEM((peers, half, lanes), jnp.bfloat16),
            pltpu.VMEM((peers, 1, 2 * half), jnp.int32),
            pltpu.VMEM((down_weight.shape[0] * lanes, 2 * width), jnp.bfloat16),
            pltpu.VMEM((half, down_weight.shape[0] * lanes), jnp.bfloat16),
            pltpu.VMEM((2 * half, 2 * width), jnp.bfloat16),
            pltpu.VMEM((coarse_count, 2 * half), jnp.bfloat16),
            pltpu.VMEM((coarse_count, 2 * width), jnp.float32),
            pltpu.SemaphoreType.DMA((peers,)),
            pltpu.SemaphoreType.DMA((peers,)),
            pltpu.SemaphoreType.DMA((peers,)),
            pltpu.SemaphoreType.DMA((peers,)),
            pltpu.SemaphoreType.DMA((2,)),
        ],
        compiler_params=pltpu.CompilerParams(
            collective_id=1, has_side_effects=True, vmem_limit_bytes=VMEM_LIMIT
        ),
        name="exchange",
    )(slots, send_sub.reshape(peers, 1, 2 * half), recv_coarse, down_weight)


def on_device(
    n_gx, n_gy,
    features, conv_weight, down_weight, kernel_map, halo_rows, send_rows, send_sub, recv_coarse,
):
    voxels, channels = features.shape
    feat_t = features.T
    halo = exchange_halo(feat_t, halo_rows, n_gx, n_gy).reshape(-1, BLOCK)
    refined_t, slots = convolve(feat_t, halo, conv_weight, kernel_map, send_rows)
    coarse = exchange_and_reduce(slots, send_sub, recv_coarse, down_weight, voxels // 4, n_gx)
    return refined_t.T, coarse


def solution(mesh):
    split = P(None, ("gx", "gy"))
    return jax.shard_map(
        functools.partial(on_device, mesh.shape["gx"], mesh.shape["gy"]),
        mesh=mesh,
        in_specs=(P(("gx", "gy"), None), P(), P(), split, split, split, split, split),
        out_specs=(P(("gx", "gy"), None), P(("gx", "gy"), None)),
        check_vma=False,
    )
```

```python
import functools

import jax
import jax.numpy as jnp
from jax import lax
from jax.experimental import pallas as pl
from jax.experimental.pallas import tpu as pltpu
from jax.sharding import PartitionSpec as P

MESH = pl.DeviceIdType.MESH
BLOCK = 128
DIRECTIONS = ((-1, -1), (-1, 0), (-1, 1), (0, -1), (0, 1), (1, -1), (1, 0), (1, 1))
VMEM_LIMIT = 60 * 1024 * 1024


def pack_kernel(halo_ref, feat_ref, out_ref):
    channels = feat_ref.shape[0]
    directions, per_direction = halo_ref.shape

    @pl.loop(0, directions)
    def _(j):
        for m in range(per_direction):
            column = pl.multiple_of(halo_ref[j, m] * BLOCK, BLOCK)
            out_ref[j, m * channels : (m + 1) * channels, :] = feat_ref[:, pl.ds(column, BLOCK)]


def halo_kernel(n_gx, n_gy, sent, out_ref, send_sem, recv_sem):
    gx, gy = lax.axis_index("gx"), lax.axis_index("gy")
    barrier = pltpu.get_barrier_semaphore()
    for dx, dy in DIRECTIONS:
        peer = (lax.rem(gx + dx + n_gx, n_gx), lax.rem(gy + dy + n_gy, n_gy))
        pl.semaphore_signal(barrier, inc=1, device_id=peer, device_id_type=MESH)
    pl.semaphore_wait(barrier, len(DIRECTIONS))

    def inside(x, y):
        return (x >= 0) & (x < n_gx) & (y >= 0) & (y < n_gy)

    def copy(j, peer):
        return pltpu.make_async_remote_copy(
            src_ref=sent.at[j],
            dst_ref=out_ref.at[j],
            send_sem=send_sem.at[j],
            recv_sem=recv_sem.at[j],
            device_id=peer,
            device_id_type=MESH,
        )

    for j, (dx, dy) in enumerate(DIRECTIONS):
        @pl.when(inside(gx + dx, gy + dy))
        def _():
            copy(j, (gx + dx, gy + dy)).start()

    for j, (dx, dy) in enumerate(DIRECTIONS):
        @pl.when(jnp.logical_not(inside(gx - dx, gy - dy)))
        def _():
            out_ref[j] = jnp.zeros(out_ref.shape[1:], out_ref.dtype)

    for j, (dx, dy) in enumerate(DIRECTIONS):
        @pl.when(inside(gx - dx, gy - dy))
        def _():
            copy(j, (gx, gy)).wait_recv()

        @pl.when(inside(gx + dx, gy + dy))
        def _():
            copy(j, (gx, gy)).wait_send()


def exchange_halo(feat_t, halo_rows, n_gx, n_gy):
    channels = feat_t.shape[0]
    directions, per_direction = halo_rows.shape
    page = (directions, per_direction * channels, BLOCK)
    vmem = pl.BlockSpec(memory_space=pltpu.VMEM)
    sent = pl.pallas_call(
        pack_kernel,
        out_shape=jax.ShapeDtypeStruct(page, feat_t.dtype),
        in_specs=[pl.BlockSpec(memory_space=pltpu.SMEM), vmem],
        out_specs=vmem,
        name="pack",
    )(halo_rows, feat_t)
    return pl.pallas_call(
        functools.partial(halo_kernel, n_gx, n_gy),
        out_shape=jax.ShapeDtypeStruct(page, feat_t.dtype),
        in_specs=[vmem],
        out_specs=vmem,
        scratch_shapes=[
            pltpu.SemaphoreType.DMA((directions,)),
            pltpu.SemaphoreType.DMA((directions,)),
        ],
        compiler_params=pltpu.CompilerParams(collective_id=0, has_side_effects=True),
        name="halo",
    )(sent)


def doubled_rows(block):
    wide = jnp.concatenate([block, block], axis=0)
    return jnp.transpose(wide)


def conv_kernel(
    group, map_ref, feat_ref, halo_ref, conv_ref, fine_out, fine, table, weights, lhs
):
    offsets, blocks = map_ref.shape
    channels, voxels = feat_ref.shape
    halo_blocks = halo_ref.shape[0] // channels
    lanes = fine.shape[1]
    pairs = (offsets + 1) // 2

    weights[...] = jnp.zeros(weights.shape, weights.dtype)
    weights[: offsets * channels, :] = jnp.concatenate([conv_ref[...], conv_ref[...]], axis=1)

    @pl.loop(0, blocks)
    def _(i):
        column = pl.multiple_of(i * BLOCK, BLOCK)
        table[pl.ds(column, BLOCK), :] = doubled_rows(feat_ref[:, pl.ds(column, BLOCK)])

    @pl.loop(0, halo_blocks)
    def _(i):
        row = pl.multiple_of((blocks + i) * BLOCK, BLOCK)
        start = pl.multiple_of(i * channels, channels)
        table[pl.ds(row, BLOCK), :] = doubled_rows(halo_ref[pl.ds(start, channels), :])

    empty = (blocks + halo_blocks) * BLOCK
    table[empty : empty + BLOCK, :] = jnp.zeros((BLOCK, lanes), table.dtype)
    fine[voxels : voxels + 8, :] = jnp.zeros((8, lanes), fine.dtype)

    low = lax.broadcasted_iota(jnp.int32, (BLOCK, lanes), 1) < channels

    def pick(k, i):
        return table[pl.ds(pl.multiple_of(map_ref[k, i] * BLOCK, BLOCK), BLOCK), :]

    @pl.loop(0, blocks // group)
    def _(g):
        for b in range(group):
            i = g * group + b
            for pair in range(pairs):
                first = pick(2 * pair, i)
                if 2 * pair + 1 < offsets:
                    both = jnp.where(low, first, pick(2 * pair + 1, i))
                else:
                    both = jnp.where(low, first, jnp.zeros_like(first))
                lhs[b * BLOCK : (b + 1) * BLOCK, pair * lanes : (pair + 1) * lanes] = both
        summed = jnp.dot(lhs[...], weights[...], preferred_element_type=jnp.float32)
        refined = jnp.maximum(summed, 0.0).astype(jnp.bfloat16).astype(jnp.float32)
        start = pl.multiple_of(g * group * BLOCK, group * BLOCK)
        fine[pl.ds(start, group * BLOCK), :] = refined
        for b in range(group):
            block = refined[b * BLOCK : (b + 1) * BLOCK, :]
            column = pl.multiple_of(start + b * BLOCK, BLOCK)
            fine_out[:, pl.ds(column, BLOCK)] = jnp.transpose(block)[:channels, :].astype(
                fine_out.dtype
            )

def convolve(feat_t, halo, conv_weight, kernel_map):
    channels, voxels = feat_t.shape
    offsets, blocks = kernel_map.shape
    group = 8
    pairs = (offsets + 1) // 2
    lanes = 2 * channels
    halo_blocks = halo.shape[0] // channels
    vmem = pl.BlockSpec(memory_space=pltpu.VMEM)
    return pl.pallas_call(
        functools.partial(conv_kernel, group),
        out_shape=(
            jax.ShapeDtypeStruct((channels, voxels), jnp.bfloat16),
            jax.ShapeDtypeStruct((voxels + 8, lanes), jnp.float32),
        ),
        in_specs=[pl.BlockSpec(memory_space=pltpu.SMEM), vmem, vmem, vmem],
        out_specs=(vmem, vmem),
        scratch_shapes=[
            pltpu.VMEM(((blocks + halo_blocks + 1) * BLOCK, lanes), jnp.bfloat16),
            pltpu.VMEM((pairs * lanes, lanes), jnp.bfloat16),
            pltpu.VMEM((group * BLOCK, pairs * lanes), jnp.bfloat16),
        ],
        compiler_params=pltpu.CompilerParams(vmem_limit_bytes=VMEM_LIMIT),
        name="convolve",
    )(kernel_map, feat_t, halo, conv_weight.reshape(offsets * channels, channels))


def torus_peer(me, depth, n_gx, step):
    spread = lax.rem(step, depth)
    odd = lax.rem(spread, 2)
    ahead = odd * ((spread + 1) // 2) + (1 - odd) * (depth - spread // 2)
    across, along = me // depth, lax.rem(me, depth)
    wide = n_gx // depth
    there = lax.rem(across + step // depth, wide)
    back = lax.rem(across - step // depth + wide, wide)
    to = there * depth + lax.rem(along + ahead, depth)
    source = back * depth + lax.rem(along - ahead + depth, depth)
    return to, source


def exchange_kernel(
    n_gx, depth, ahead,
    rows_ref, fine, sub_ref, coarse_ref, down_ref, coarse_out,
    stage, packed, own_codes,
    landed, codes, wide, placed, terms, hot, total,
    row_send, row_recv, code_send, code_recv,
):
    me, gy = lax.axis_index("gx"), lax.axis_index("gy")
    peers, half, lanes = packed.shape
    capacity = 2 * half
    subs, channels, width = down_ref.shape
    coarse_count = coarse_out.shape[0]
    zero, one = jnp.bfloat16(0), jnp.bfloat16(1)

    barrier = pltpu.get_barrier_semaphore()

    @pl.loop(1, n_gx)
    def _(step):
        to, source = torus_peer(me, depth, n_gx, step)
        pl.semaphore_signal(barrier, inc=1, device_id=(to, gy), device_id_type=MESH)

    wide[...] = jnp.zeros(wide.shape, wide.dtype)
    for s in range(subs):
        wide[s * lanes : s * lanes + channels, :width] = down_ref[s]
        wide[s * lanes + channels : (s + 1) * lanes, width:] = down_ref[s]
    total[...] = jnp.zeros(total.shape, total.dtype)
    for p in range(peers):
        own_codes[p] = sub_ref[p : p + 1, :]

    low_row = lax.broadcasted_iota(jnp.int32, (1, lanes), 1) < channels
    low_half = lax.broadcasted_iota(jnp.int32, (half, lanes), 1) < channels
    ids = lax.broadcasted_iota(jnp.int32, (BLOCK, capacity), 0).astype(jnp.bfloat16)

    def gather(step):
        to, source = torus_peer(me, depth, n_gx, step)
        base = to * capacity
        for c in range(half):
            first = fine[pl.ds(rows_ref[base + c], 1), :]
            second = fine[pl.ds(rows_ref[base + half + c], 1), :]
            stage[c : c + 1, :] = jnp.where(low_row, first, second)
        packed[step] = stage[...].astype(packed.dtype)

    def rows_copy(step, to):
        return pltpu.make_async_remote_copy(
            src_ref=packed.at[step],
            dst_ref=landed.at[step],
            send_sem=row_send.at[step],
            recv_sem=row_recv.at[step],
            device_id=(to, gy),
            device_id_type=MESH,
        )

    def codes_copy(step, to):
        return pltpu.make_async_remote_copy(
            src_ref=own_codes.at[to],
            dst_ref=codes.at[step],
            send_sem=code_send.at[step],
            recv_sem=code_recv.at[step],
            device_id=(to, gy),
            device_id_type=MESH,
        )

    def send(step):
        to, source = torus_peer(me, depth, n_gx, step)
        codes_copy(step, to).start()
        rows_copy(step, to).start()

    def reduce(step, rows, code):
        to, source = torus_peer(me, depth, n_gx, step)
        target = coarse_ref[pl.ds(source, 1), :]
        part = target // BLOCK
        lower = target - part * BLOCK
        upper = part // 8
        part = part - upper * 8
        mark = (code + subs * upper).astype(jnp.float32).astype(jnp.bfloat16)
        first = jnp.transpose(jnp.broadcast_to(mark[:, :half], (lanes, half)))
        second = jnp.transpose(jnp.broadcast_to(mark[:, half:], (lanes, half)))
        edge = jnp.bfloat16(subs)
        first_up, second_up = first >= edge, second >= edge
        column = jnp.where(
            low_half,
            jnp.where(first_up, first - edge, first),
            jnp.where(second_up, second - edge, second),
        )
        for s in range(subs):
            placed[:, s * lanes : (s + 1) * lanes] = jnp.where(
                column == jnp.bfloat16(s), rows, jnp.zeros_like(rows)
            )
        product = jnp.dot(placed[...], wide[...], preferred_element_type=jnp.float32)
        product = product.astype(jnp.bfloat16)
        terms[:half, :width] = jnp.where(first_up, zero, product[:, :width])
        terms[:half, width:] = jnp.where(first_up, product[:, :width], zero)
        terms[half:, :width] = jnp.where(second_up, zero, product[:, width:])
        terms[half:, width:] = jnp.where(second_up, product[:, width:], zero)
        for h in range(coarse_count // 2 // BLOCK):
            wanted = jnp.where(part == h, lower, -1).astype(jnp.float32).astype(jnp.bfloat16)
            hot[h * BLOCK : (h + 1) * BLOCK, :] = jnp.where(ids == wanted, one, zero)
        total[...] += jnp.dot(hot[...], terms[...], preferred_element_type=jnp.float32)

    pl.semaphore_wait(barrier, n_gx - 1)

    gather(1)

    @pl.loop(2, ahead + 1)
    def _(step):
        gather(step)
        send(step - 1)

    gather(0)
    send(ahead)

    gather(ahead + 1)
    reduce(0, packed[0], own_codes[me])

    @pl.loop(1, n_gx - ahead - 1)
    def _(step):
        send(step + ahead)
        codes_copy(step, me).wait_recv()
        rows_copy(step, me).wait_recv()
        gather(step + ahead + 1)
        reduce(step, landed[step], codes[step])

    send(n_gx - 1)

    @pl.loop(n_gx - ahead - 1, n_gx)
    def _(step):
        codes_copy(step, me).wait_recv()
        rows_copy(step, me).wait_recv()
        reduce(step, landed[step], codes[step])

    coarse_out[: coarse_count // 2, :] = total[:, :width].astype(coarse_out.dtype)
    coarse_out[coarse_count // 2 :, :] = total[:, width:].astype(coarse_out.dtype)

    @pl.loop(1, n_gx)
    def _(step):
        codes_copy(step, me).wait_send()
        rows_copy(step, me).wait_send()


def exchange_and_reduce(fine, down_weight, send_rows, send_sub, recv_coarse, coarse_count, n_gx):
    peers, capacity = send_rows.shape
    subs, channels, width = down_weight.shape
    depth, ahead = 8, 16
    half, lanes = capacity // 2, 2 * channels
    vmem = pl.BlockSpec(memory_space=pltpu.VMEM)
    smem = pl.BlockSpec(memory_space=pltpu.SMEM)
    bf16 = jnp.bfloat16
    return pl.pallas_call(
        functools.partial(exchange_kernel, n_gx, depth, ahead),
        out_shape=jax.ShapeDtypeStruct((coarse_count, width), bf16),
        in_specs=[smem, vmem, vmem, vmem, vmem],
        out_specs=vmem,
        scratch_shapes=[
            pltpu.VMEM((half, lanes), jnp.float32),
            pltpu.VMEM((peers, half, lanes), bf16),
            pltpu.VMEM((peers, 1, capacity), jnp.int32),
            pltpu.VMEM((peers, half, lanes), bf16),
            pltpu.VMEM((peers, 1, capacity), jnp.int32),
            pltpu.VMEM((subs * lanes, 2 * width), bf16),
            pltpu.VMEM((half, subs * lanes), bf16),
            pltpu.VMEM((capacity, 2 * width), bf16),
            pltpu.VMEM((coarse_count // 2, capacity), bf16),
            pltpu.VMEM((coarse_count // 2, 2 * width), jnp.float32),
            pltpu.SemaphoreType.DMA((peers,)),
            pltpu.SemaphoreType.DMA((peers,)),
            pltpu.SemaphoreType.DMA((peers,)),
            pltpu.SemaphoreType.DMA((peers,)),
        ],
        compiler_params=pltpu.CompilerParams(
            collective_id=1, has_side_effects=True, vmem_limit_bytes=VMEM_LIMIT
        ),
        name="exchange",
    )(send_rows.reshape(-1), fine, send_sub, recv_coarse, down_weight)


def on_device(
    n_gx, n_gy,
    features, conv_weight, down_weight, kernel_map, halo_rows, send_rows, send_sub, recv_coarse,
):
    voxels, channels = features.shape
    feat_t = features.T
    halo = exchange_halo(feat_t, halo_rows, n_gx, n_gy).reshape(-1, BLOCK)
    refined_t, fine = convolve(feat_t, halo, conv_weight, kernel_map)
    coarse = exchange_and_reduce(
        fine, down_weight, send_rows, send_sub, recv_coarse, voxels // 4, n_gx
    )
    return refined_t.T, coarse


def solution(mesh):
    split = P(None, ("gx", "gy"))
    return jax.shard_map(
        functools.partial(on_device, mesh.shape["gx"], mesh.shape["gy"]),
        mesh=mesh,
        in_specs=(P(("gx", "gy"), None), P(), P(), split, split, split, split, split),
        out_specs=(P(("gx", "gy"), None), P(("gx", "gy"), None)),
        check_vma=False,
    )
```

```python
import functools

import jax
import jax.numpy as jnp
from jax import lax
from jax.experimental import pallas as pl
from jax.experimental.pallas import tpu as pltpu
from jax.sharding import PartitionSpec as P

MESH = pl.DeviceIdType.MESH
BLOCK = 128
DIRECTIONS = ((-1, -1), (-1, 0), (-1, 1), (0, -1), (0, 1), (1, -1), (1, 0), (1, 1))
VMEM_LIMIT = 60 * 1024 * 1024


def pack_kernel(halo_ref, feat_ref, out_ref):
    channels = feat_ref.shape[0]
    directions, per_direction = halo_ref.shape

    @pl.loop(0, directions)
    def _(j):
        for m in range(per_direction):
            column = pl.multiple_of(halo_ref[j, m] * BLOCK, BLOCK)
            out_ref[j, m * channels : (m + 1) * channels, :] = feat_ref[:, pl.ds(column, BLOCK)]


def halo_kernel(n_gx, n_gy, sent, out_ref, send_sem, recv_sem):
    gx, gy = lax.axis_index("gx"), lax.axis_index("gy")
    barrier = pltpu.get_barrier_semaphore()
    for dx, dy in DIRECTIONS:
        peer = (lax.rem(gx + dx + n_gx, n_gx), lax.rem(gy + dy + n_gy, n_gy))
        pl.semaphore_signal(barrier, inc=1, device_id=peer, device_id_type=MESH)
    pl.semaphore_wait(barrier, len(DIRECTIONS))

    def inside(x, y):
        return (x >= 0) & (x < n_gx) & (y >= 0) & (y < n_gy)

    def copy(j, peer):
        return pltpu.make_async_remote_copy(
            src_ref=sent.at[j],
            dst_ref=out_ref.at[j],
            send_sem=send_sem.at[j],
            recv_sem=recv_sem.at[j],
            device_id=peer,
            device_id_type=MESH,
        )

    for j, (dx, dy) in enumerate(DIRECTIONS):
        @pl.when(inside(gx + dx, gy + dy))
        def _():
            copy(j, (gx + dx, gy + dy)).start()

    for j, (dx, dy) in enumerate(DIRECTIONS):
        @pl.when(jnp.logical_not(inside(gx - dx, gy - dy)))
        def _():
            out_ref[j] = jnp.zeros(out_ref.shape[1:], out_ref.dtype)

    for j, (dx, dy) in enumerate(DIRECTIONS):
        @pl.when(inside(gx - dx, gy - dy))
        def _():
            copy(j, (gx, gy)).wait_recv()

        @pl.when(inside(gx + dx, gy + dy))
        def _():
            copy(j, (gx, gy)).wait_send()


def exchange_halo(feat_t, halo_rows, n_gx, n_gy):
    channels = feat_t.shape[0]
    directions, per_direction = halo_rows.shape
    page = (directions, per_direction * channels, BLOCK)
    vmem = pl.BlockSpec(memory_space=pltpu.VMEM)
    sent = pl.pallas_call(
        pack_kernel,
        out_shape=jax.ShapeDtypeStruct(page, feat_t.dtype),
        in_specs=[pl.BlockSpec(memory_space=pltpu.SMEM), vmem],
        out_specs=vmem,
        name="pack",
    )(halo_rows, feat_t)
    return pl.pallas_call(
        functools.partial(halo_kernel, n_gx, n_gy),
        out_shape=jax.ShapeDtypeStruct(page, feat_t.dtype),
        in_specs=[vmem],
        out_specs=vmem,
        scratch_shapes=[
            pltpu.SemaphoreType.DMA((directions,)),
            pltpu.SemaphoreType.DMA((directions,)),
        ],
        compiler_params=pltpu.CompilerParams(collective_id=0, has_side_effects=True),
        name="halo",
    )(sent)


def conv_kernel(
    group, map_ref, feat_ref, halo_ref, conv_ref, fine_out, fine, table, weights, picked
):
    offsets, blocks = map_ref.shape
    channels, voxels = feat_ref.shape
    lanes = fine.shape[1]
    weights[...] = jnp.transpose(conv_ref[...])
    for i in range(blocks):
        table[i] = feat_ref[:, i * BLOCK : (i + 1) * BLOCK]
    for i in range(blocks, table.shape[0] - 1):
        start = (i - blocks) * channels
        table[i] = halo_ref[start : start + channels, :]
    table[table.shape[0] - 1] = jnp.zeros(table.shape[1:], table.dtype)
    fine[voxels : voxels + 8, :] = jnp.zeros((8, lanes), fine.dtype)

    @pl.loop(0, blocks // group)
    def _(g):
        for k in range(offsets):
            for b in range(group):
                picked[k * channels : (k + 1) * channels, b * BLOCK : (b + 1) * BLOCK] = table[
                    map_ref[k, g * group + b]
                ]
        summed = jnp.dot(weights[...], picked[...], preferred_element_type=jnp.float32)
        refined = jnp.maximum(summed, 0.0).astype(jnp.bfloat16)
        start = pl.multiple_of(g * group * BLOCK, group * BLOCK)
        fine_out[:, pl.ds(start, group * BLOCK)] = refined
        for b in range(group):
            block = refined[:, b * BLOCK : (b + 1) * BLOCK].astype(jnp.float32)
            row = pl.multiple_of(start + b * BLOCK, BLOCK)
            fine[pl.ds(row, BLOCK), :] = jnp.transpose(jnp.concatenate([block, block], axis=0))


def convolve(feat_t, halo, conv_weight, kernel_map):
    channels, voxels = feat_t.shape
    offsets, blocks = kernel_map.shape
    group = 32
    lanes = 2 * channels
    halo_blocks = halo.shape[0] // channels
    vmem = pl.BlockSpec(memory_space=pltpu.VMEM)
    return pl.pallas_call(
        functools.partial(conv_kernel, group),
        out_shape=(
            jax.ShapeDtypeStruct((channels, voxels), jnp.bfloat16),
            jax.ShapeDtypeStruct((voxels + 8, lanes), jnp.float32),
        ),
        in_specs=[pl.BlockSpec(memory_space=pltpu.SMEM), vmem, vmem, vmem],
        out_specs=(vmem, vmem),
        scratch_shapes=[
            pltpu.VMEM((blocks + halo_blocks + 1, channels, BLOCK), jnp.bfloat16),
            pltpu.VMEM((channels, offsets * channels), jnp.bfloat16),
            pltpu.VMEM((offsets * channels, group * BLOCK), jnp.bfloat16),
        ],
        compiler_params=pltpu.CompilerParams(vmem_limit_bytes=VMEM_LIMIT),
        name="convolve",
    )(kernel_map, feat_t, halo, conv_weight.reshape(offsets * channels, channels))


def torus_peer(me, depth, n_gx, step):
    spread = lax.rem(step, depth)
    odd = lax.rem(spread, 2)
    ahead = odd * ((spread + 1) // 2) + (1 - odd) * (depth - spread // 2)
    across, along = me // depth, lax.rem(me, depth)
    wide = n_gx // depth
    there = lax.rem(across + step // depth, wide)
    back = lax.rem(across - step // depth + wide, wide)
    to = there * depth + lax.rem(along + ahead, depth)
    source = back * depth + lax.rem(along - ahead + depth, depth)
    return to, source


def exchange_kernel(
    n_gx, depth, ahead,
    rows_ref, fine, sub_ref, coarse_ref, down_ref, coarse_out,
    stage, packed, own_codes,
    landed, codes, wide, placed, terms, hot, total,
    row_send, row_recv, code_send, code_recv,
):
    me, gy = lax.axis_index("gx"), lax.axis_index("gy")
    peers, half, lanes = packed.shape
    capacity = 2 * half
    subs, channels, width = down_ref.shape
    coarse_count = coarse_out.shape[0]
    zero, one = jnp.bfloat16(0), jnp.bfloat16(1)

    barrier = pltpu.get_barrier_semaphore()

    @pl.loop(1, n_gx)
    def _(step):
        to, source = torus_peer(me, depth, n_gx, step)
        pl.semaphore_signal(barrier, inc=1, device_id=(to, gy), device_id_type=MESH)

    wide[...] = jnp.zeros(wide.shape, wide.dtype)
    for s in range(subs):
        wide[s * lanes : s * lanes + channels, :width] = down_ref[s]
        wide[s * lanes + channels : (s + 1) * lanes, width:] = down_ref[s]
    total[...] = jnp.zeros(total.shape, total.dtype)
    for p in range(peers):
        own_codes[p] = sub_ref[p : p + 1, :]

    low_row = lax.broadcasted_iota(jnp.int32, (1, lanes), 1) < channels
    low_half = lax.broadcasted_iota(jnp.int32, (half, lanes), 1) < channels
    ids = lax.broadcasted_iota(jnp.int32, (BLOCK, capacity), 0).astype(jnp.bfloat16)

    def gather(step):
        to, source = torus_peer(me, depth, n_gx, step)
        base = to * capacity
        for c in range(half):
            first = fine[pl.ds(rows_ref[base + c], 1), :]
            second = fine[pl.ds(rows_ref[base + half + c], 1), :]
            stage[c : c + 1, :] = jnp.where(low_row, first, second)
        packed[step] = stage[...].astype(packed.dtype)

    def rows_copy(step, to):
        return pltpu.make_async_remote_copy(
            src_ref=packed.at[step],
            dst_ref=landed.at[step],
            send_sem=row_send.at[step],
            recv_sem=row_recv.at[step],
            device_id=(to, gy),
            device_id_type=MESH,
        )

    def codes_copy(step, to):
        return pltpu.make_async_remote_copy(
            src_ref=own_codes.at[to],
            dst_ref=codes.at[step],
            send_sem=code_send.at[step],
            recv_sem=code_recv.at[step],
            device_id=(to, gy),
            device_id_type=MESH,
        )

    def send(step):
        to, source = torus_peer(me, depth, n_gx, step)
        codes_copy(step, to).start()
        rows_copy(step, to).start()

    def reduce(step, rows, code):
        to, source = torus_peer(me, depth, n_gx, step)
        target = coarse_ref[pl.ds(source, 1), :]
        part = target // BLOCK
        lower = target - part * BLOCK
        upper = part // 8
        part = part - upper * 8
        mark = (code + subs * upper).astype(jnp.float32).astype(jnp.bfloat16)
        first = jnp.transpose(jnp.broadcast_to(mark[:, :half], (lanes, half)))
        second = jnp.transpose(jnp.broadcast_to(mark[:, half:], (lanes, half)))
        edge = jnp.bfloat16(subs)
        first_up, second_up = first >= edge, second >= edge
        column = jnp.where(
            low_half,
            jnp.where(first_up, first - edge, first),
            jnp.where(second_up, second - edge, second),
        )
        for s in range(subs):
            placed[:, s * lanes : (s + 1) * lanes] = jnp.where(
                column == jnp.bfloat16(s), rows, jnp.zeros_like(rows)
            )
        product = jnp.dot(placed[...], wide[...], preferred_element_type=jnp.float32)
        product = product.astype(jnp.bfloat16)
        terms[:half, :width] = jnp.where(first_up, zero, product[:, :width])
        terms[:half, width:] = jnp.where(first_up, product[:, :width], zero)
        terms[half:, :width] = jnp.where(second_up, zero, product[:, width:])
        terms[half:, width:] = jnp.where(second_up, product[:, width:], zero)
        for h in range(coarse_count // 2 // BLOCK):
            wanted = jnp.where(part == h, lower, -1).astype(jnp.float32).astype(jnp.bfloat16)
            hot[h * BLOCK : (h + 1) * BLOCK, :] = jnp.where(ids == wanted, one, zero)
        total[...] += jnp.dot(hot[...], terms[...], preferred_element_type=jnp.float32)

    pl.semaphore_wait(barrier, n_gx - 1)

    gather(1)

    @pl.loop(2, ahead + 1)
    def _(step):
        gather(step)
        send(step - 1)

    gather(0)
    send(ahead)

    gather(ahead + 1)
    reduce(0, packed[0], own_codes[me])

    @pl.loop(1, n_gx - ahead - 1)
    def _(step):
        send(step + ahead)
        codes_copy(step, me).wait_recv()
        rows_copy(step, me).wait_recv()
        gather(step + ahead + 1)
        reduce(step, landed[step], codes[step])

    send(n_gx - 1)

    @pl.loop(n_gx - ahead - 1, n_gx)
    def _(step):
        codes_copy(step, me).wait_recv()
        rows_copy(step, me).wait_recv()
        reduce(step, landed[step], codes[step])

    coarse_out[: coarse_count // 2, :] = total[:, :width].astype(coarse_out.dtype)
    coarse_out[coarse_count // 2 :, :] = total[:, width:].astype(coarse_out.dtype)

    @pl.loop(1, n_gx)
    def _(step):
        codes_copy(step, me).wait_send()
        rows_copy(step, me).wait_send()


def exchange_and_reduce(fine, down_weight, send_rows, send_sub, recv_coarse, coarse_count, n_gx):
    peers, capacity = send_rows.shape
    subs, channels, width = down_weight.shape
    depth, ahead = 8, 16
    half, lanes = capacity // 2, 2 * channels
    vmem = pl.BlockSpec(memory_space=pltpu.VMEM)
    smem = pl.BlockSpec(memory_space=pltpu.SMEM)
    bf16 = jnp.bfloat16
    return pl.pallas_call(
        functools.partial(exchange_kernel, n_gx, depth, ahead),
        out_shape=jax.ShapeDtypeStruct((coarse_count, width), bf16),
        in_specs=[smem, vmem, vmem, vmem, vmem],
        out_specs=vmem,
        scratch_shapes=[
            pltpu.VMEM((half, lanes), jnp.float32),
            pltpu.VMEM((peers, half, lanes), bf16),
            pltpu.VMEM((peers, 1, capacity), jnp.int32),
            pltpu.VMEM((peers, half, lanes), bf16),
            pltpu.VMEM((peers, 1, capacity), jnp.int32),
            pltpu.VMEM((subs * lanes, 2 * width), bf16),
            pltpu.VMEM((half, subs * lanes), bf16),
            pltpu.VMEM((capacity, 2 * width), bf16),
            pltpu.VMEM((coarse_count // 2, capacity), bf16),
            pltpu.VMEM((coarse_count // 2, 2 * width), jnp.float32),
            pltpu.SemaphoreType.DMA((peers,)),
            pltpu.SemaphoreType.DMA((peers,)),
            pltpu.SemaphoreType.DMA((peers,)),
            pltpu.SemaphoreType.DMA((peers,)),
        ],
        compiler_params=pltpu.CompilerParams(
            collective_id=1, has_side_effects=True, vmem_limit_bytes=VMEM_LIMIT
        ),
        name="exchange",
    )(send_rows.reshape(-1), fine, send_sub, recv_coarse, down_weight)


def on_device(
    n_gx, n_gy,
    features, conv_weight, down_weight, kernel_map, halo_rows, send_rows, send_sub, recv_coarse,
):
    voxels, channels = features.shape
    feat_t = features.T
    halo = exchange_halo(feat_t, halo_rows, n_gx, n_gy).reshape(-1, BLOCK)
    refined_t, fine = convolve(feat_t, halo, conv_weight, kernel_map)
    coarse = exchange_and_reduce(
        fine, down_weight, send_rows, send_sub, recv_coarse, voxels // 4, n_gx
    )
    return refined_t.T, coarse


def solution(mesh):
    split = P(None, ("gx", "gy"))
    return jax.shard_map(
        functools.partial(on_device, mesh.shape["gx"], mesh.shape["gy"]),
        mesh=mesh,
        in_specs=(P(("gx", "gy"), None), P(), P(), split, split, split, split, split),
        out_specs=(P(("gx", "gy"), None), P(("gx", "gy"), None)),
        check_vma=False,
    )
```
